32 devices in a mesh: seq: 2 (over x), ctx: 8 (over z, core), tensor: 2 (over y).
Axes of the slice: x: 2, y: 2, z: 4, core: 2. Of those that a mesh axis runs over, the one named last changes fastest.
Arguments:
- block_input: bfloat16 [4, 512, 1024], P('seq', 'ctx'), may hold values from -6 to 6
- cotangent: bfloat16 [4, 512, 1024], P('seq', 'ctx'), may hold values from -6 to 6
- block_order: int32 [4, 8], P('seq'), may hold values from 0 to 7, each once within a row
- routes: int32 [4, 512, 8], P('seq', 'ctx'), may hold values from 0 to 15, all different within a row; in each aligned block of 64 rows (0 to 63, 64 to 127, ..., all dimensions but the last counted through in order) at most 40 rows name the same one
- route_weights: bfloat16 [4, 512, 8], P('seq', 'ctx'), may hold values from 0.049804688 to 0.29882812
- gain_attn: bfloat16 [1024], P('seq'), may hold values from 0.5 to 1.5
- w_query: bfloat16 [1024, 1024], P('seq', 'tensor'), may hold values from -40 to 40
- key_weight: bfloat16 [1024, 512], P('seq', 'tensor'), may hold values from -0.1875 to 0.1875
- value_weight: bfloat16 [1024, 512], P('seq', 'tensor'), may hold values from -0.1875 to 0.1875
- w_out: bfloat16 [1024, 1024], P('tensor', 'seq'), may hold values from -6 to 6
- gain_moe: bfloat16 [1024], P('seq'), may hold values from 0.5 to 1.5
- w_gate: bfloat16 [16, 1024, 512], P('seq', None, 'tensor'), may hold values from -0.1875 to 0.1875
- w_up: bfloat16 [16, 1024, 512], P('seq', None, 'tensor'), may hold values from -0.1875 to 0.1875
- w_down: bfloat16 [16, 512, 1024], P('seq', 'tensor'), may hold values from -2 to 2
Outputs:
- block_output: bfloat16 [4, 512, 1024], P('seq', 'ctx')
- input_grad: float32 [4, 512, 1024], P('seq', 'ctx')
- grad_gain_attn: float32 [1024], P('seq')
- grad_query: float32 [1024, 1024], P('seq', 'tensor')
- grad_key: float32 [1024, 512], P('seq', 'tensor')
- grad_value: float32 [1024, 512], P('seq', 'tensor')
- grad_out: float32 [1024, 1024], P('tensor', 'seq')
- grad_gain_moe: float32 [1024], P('seq')
- grad_gate: float32 [16, 1024, 512], P('seq', 'ctx', 'tensor')
- grad_up: float32 [16, 1024, 512], P('seq', 'ctx', 'tensor')
- grad_down: float32 [16, 512, 1024], P('seq', 'tensor', 'ctx')
The draws below stay inside these ranges and needn't reach their ends.
Inputs may be any that keep to these rules, and one draw needn't show every extreme that they name: `routes`: within the 64 stored tokens of one sequence on one ctx index, no expert is chosen by more than 40 tokens, and one expert is chosen by exactly 40. Each row is a permutation; the stored block j of a sequence holds the positions block_order[j] * 64 to block_order[j] * 64 + 63 in order.
All inputs are finite; a program needn't handle non-finite values.
Results may differ from the reference program's by a relative error of at most 0.03.
Values may be sent and summed in bfloat16 or wider, within the bound.
No kernel may reach another device: no remote copies, remote signals or barrier semaphores. Data moves between devices by JAX's collectives and lax.ppermute only.
A program may use at most 256 MiB of HBM per device.

```python
import math
import jax
import jax.numpy as jnp
import numpy as np
from jax import lax

MODEL_DIM = 1024
QUERY_HEADS = 16
KEY_VALUE_HEADS = 8
HEAD_DIM = 64
EXPERT_HIDDEN = 512
TOPK = 8
LOCAL_EXPERTS = 16
CTX_TOK = 64
CAP = 40
SEQUENCE_TOKENS = 512
SEQS = 4
N_CTX = 8


def draw_w_query(key, part):
    base = jnp.clip(jax.random.normal(jax.random.fold_in(key, 11), (MODEL_DIM, QUERY_HEADS * HEAD_DIM), jnp.float32), -6.0, 6.0)
    head_scale = jnp.exp(jax.random.uniform(jax.random.fold_in(key, 12), (QUERY_HEADS, 1), jnp.float32, -0.7, 0.7))
    columns = jnp.broadcast_to(head_scale, (QUERY_HEADS, HEAD_DIM)).reshape(1, QUERY_HEADS * HEAD_DIM)
    return (base * columns * 0.25).astype(jnp.bfloat16)


def levels(stream_key, dims, pieces, low, largest):
    def one(axis_at, shards_of):
        draws = jax.random.uniform(jax.random.fold_in(jax.random.fold_in(stream_key, 6), axis_at), (shards_of,), jnp.float32, low / len(pieces), largest / len(pieces))
        return jnp.repeat(jnp.exp(draws), dims[axis_at] // shards_of).reshape((-1,) + (1,) * (len(dims) - axis_at - 1))

    gain = one(*pieces[0])
    for cut in pieces[1:]:
        gain = gain * one(*cut)
    return gain


def shared_out(stream_key, own, number, rows, count, top, reach, slope):
    order = jax.random.permutation(stream_key, count)
    packed, usual = load_shares(count, rows * top, reach, slope, True), load_shares(count, rows * top, reach, slope, False)
    places = jnp.arange(count)

    def named(lengths, turn):
        used = int((lengths > 0).sum())
        fixed = max(1, used // 4)
        moved = fixed + (places - fixed + turn * (used - fixed)) % max(1, count - fixed)
        return jnp.zeros((count,), jnp.int32).at[order[jnp.where(places < fixed, places, moved)]].set(jnp.asarray(lengths, jnp.int32))

    lengths = jnp.where(number % 4 == 0, named(packed, number // 4), named(usual, number - number // 4 - 1))
    mixed = jax.random.permutation(jax.random.fold_in(own, 3), count)
    source_of, taker = mixed[0:count // 2 * 2:2], mixed[1:count // 2 * 2:2]
    margin = jnp.minimum(lengths[source_of] - 1, reach - lengths[taker]) // 2
    margin = jnp.where((source_of == order[0]) | (taker == order[0]) | (lengths[taker] == 0), 0, jnp.maximum(margin, 0))
    moved = jax.random.randint(jax.random.fold_in(own, 4), (count // 2,), 0, 1 << 20) % (margin + 1)
    lengths = lengths.at[source_of].add(-moved).at[taker].add(moved)
    items = jnp.searchsorted(jnp.cumsum(lengths), jnp.arange(rows * top), side="right").astype(jnp.int32)
    listing = items.reshape(top, rows).T
    listing = listing[jax.random.permutation(jax.random.fold_in(own, 1), rows)]
    turn = jax.random.randint(jax.random.fold_in(own, 2), (rows, 1), 0, top)
    return jnp.take_along_axis(listing, (jnp.arange(top)[None, :] + turn) % top, axis=1)


def load_shares(amount, total, reach, slope, full):
    loads = [(1 << 20) // math.isqrt(standing ** slope) + 1 for standing in range(1, amount + 1)]
    largest = reach if full else min(reach, max(-(-total // amount), total * loads[0] // sum(loads)))
    least = 1 if total - largest >= amount - 1 else 0
    given, spare = [largest] + [least] * (amount - 1), total - largest - least * (amount - 1)
    while spare > 0:
        movable = [i for i in range(1, amount) if given[i] < largest] or [i for i in range(1, amount) if given[i] < reach]
        mass, remaining = sum([loads[i] for i in movable]), spare
        for i in movable:
            extra = min(reach - given[i], max(1, remaining * loads[i] // mass), spare)
            given[i] = given[i] + extra
            spare = spare - extra
    return np.array(given)


def gaussian(own_key, extent, deviation, limit, shards=(), kind=jnp.bfloat16):
    array = jax.random.normal(own_key, extent, jnp.float32) * deviation
    if len(shards) > 0:
        array = levels(own_key, extent, shards, -0.22, 0.18) * array
    return jnp.clip(array, min=-limit, max=limit).astype(kind)


def setup_inputs(seed: int = 0) -> dict:
    keys = jax.random.split(jax.random.key(seed), 15)
    block_input = gaussian(keys[0], (SEQS, SEQUENCE_TOKENS, MODEL_DIM), 1.0, 6.0, ((0, 2), (1, 8)))
    cotangent = gaussian(keys[1], (SEQS, SEQUENCE_TOKENS, MODEL_DIM), 1.0, 6.0, ((0, 2), (1, 8)))
    block_order = jax.vmap(lambda own: jax.random.permutation(own, N_CTX))(jax.random.split(keys[2], SEQS)).reshape((SEQS, N_CTX)).astype(jnp.int32)
    routes_keys = jax.random.split(jax.random.fold_in(keys[3], 1), SEQS * SEQUENCE_TOKENS // CTX_TOK)
    routes_turns = jax.random.permutation(jax.random.fold_in(keys[3], 3), SEQS * SEQUENCE_TOKENS // CTX_TOK)
    routes = jax.vmap(lambda own, number: shared_out(jax.random.fold_in(keys[3], 2), own, number, CTX_TOK, LOCAL_EXPERTS, TOPK, CAP, 2))(routes_keys, routes_turns).reshape((SEQS, SEQUENCE_TOKENS, TOPK))
    route_weights = jnp.clip(0.049804688 + 0.24902344 * jax.random.uniform(keys[4], (SEQS, SEQUENCE_TOKENS, TOPK), jnp.float32) ** levels(keys[4], (SEQS, SEQUENCE_TOKENS, TOPK), ((0, 2), (1, 8)), -0.2, 0.2), 0.049804688, 0.29882812).astype(jnp.bfloat16)
    gain_attn = jnp.clip(1.0 + 0.1 * jax.random.normal(keys[5], (MODEL_DIM,), jnp.float32), 0.5, 1.5).astype(jnp.bfloat16)
    w_query = draw_w_query(jax.random.fold_in(keys[14], 71), 0)
    key_weight = gaussian(keys[7], (MODEL_DIM, KEY_VALUE_HEADS * HEAD_DIM), MODEL_DIM ** -0.5, 0.1875, ((0, 2), (1, 2)))
    value_weight = gaussian(keys[8], (MODEL_DIM, KEY_VALUE_HEADS * HEAD_DIM), MODEL_DIM ** -0.5, 0.1875, ((0, 2), (1, 2)))
    w_out = gaussian(keys[9], (QUERY_HEADS * HEAD_DIM, MODEL_DIM), (max(1, QUERY_HEADS * HEAD_DIM // 1024)) ** -0.5, 6.0, ((0, 2), (1, 2)))
    gain_moe = jnp.clip(1.0 + 0.1 * jax.random.normal(keys[10], (MODEL_DIM,), jnp.float32), 0.5, 1.5).astype(jnp.bfloat16)
    w_gate = gaussian(keys[11], (LOCAL_EXPERTS, MODEL_DIM, EXPERT_HIDDEN), MODEL_DIM ** -0.5, 0.1875, ((0, 2), (2, 2)))
    w_up = gaussian(keys[12], (LOCAL_EXPERTS, MODEL_DIM, EXPERT_HIDDEN), MODEL_DIM ** -0.5, 0.1875, ((0, 2), (2, 2)))
    w_down = gaussian(keys[13], (LOCAL_EXPERTS, EXPERT_HIDDEN, MODEL_DIM), (max(1, EXPERT_HIDDEN // 64)) ** -0.5, 2.0, ((0, 2), (1, 2)))
    return {"block_input": block_input, "cotangent": cotangent, "block_order": block_order, "routes": routes, "route_weights": route_weights, "gain_attn": gain_attn, "w_query": w_query, "key_weight": key_weight, "value_weight": value_weight, "w_out": w_out, "gain_moe": gain_moe, "w_gate": w_gate, "w_up": w_up, "w_down": w_down}


EPS = 1e-06
SCORE_SCALE = 1.0 / 64.0
RESIDUAL_SCALE = 0.22
THETA = 10000.0
NEG_FILL = -1e+30

def round_trip(values):
    return lax.optimization_barrier(values.astype(jnp.bfloat16)).astype(jnp.float32)

def rope_tables(positions):
    half_dim = HEAD_DIM // 2
    exponent = jnp.arange(half_dim, dtype=jnp.float32) * (2.0 / HEAD_DIM)
    frequency = THETA ** (-exponent)
    angles = positions.astype(jnp.float32)[..., None] * frequency
    return (jnp.cos(angles), jnp.sin(angles))

def apply_rotary(values, cosine_table, sine_values):
    half_dim = HEAD_DIM // 2
    lower_half = values[..., :half_dim]
    upper_half = values[..., half_dim:]
    return jnp.concatenate([lower_half * cosine_table - upper_half * sine_values, upper_half * cosine_table + lower_half * sine_values], axis=-1)

def inverse_rotary(grad_vals, cosine_table, sine_values):
    half_dim = HEAD_DIM // 2
    lower_half = grad_vals[..., :half_dim]
    upper_half = grad_vals[..., half_dim:]
    return jnp.concatenate([lower_half * cosine_table + upper_half * sine_values, upper_half * cosine_table - lower_half * sine_values], axis=-1)

def expert_slots(route_rows, capacity):
    row_total = route_rows.shape[0]
    flat_routes = route_rows.reshape(-1).astype(jnp.int32)
    one_hot = (flat_routes[:, None] == jnp.arange(LOCAL_EXPERTS, dtype=jnp.int32)[None, :]).astype(jnp.int32)
    slot_rank = (jnp.cumsum(one_hot, axis=0) - one_hot).astype(jnp.int32)
    slot_of = (lax.optimization_barrier(jnp.sum(slot_rank * one_hot, axis=1)).astype(jnp.int32) + flat_routes * capacity).astype(jnp.int32)
    slot_owner = jnp.full((LOCAL_EXPERTS * capacity,), row_total, jnp.int32)
    slot_owner = slot_owner.at[slot_of].set((jnp.arange(row_total * TOPK, dtype=jnp.int32) // TOPK).astype(jnp.int32))
    return (slot_of.reshape(row_total, TOPK), slot_owner)

def attend_forward(query_rotated, key_rot, value_b, positions):
    heads_per_group = QUERY_HEADS // KEY_VALUE_HEADS
    block_tokens = min(SEQUENCE_TOKENS, 512)
    number_of_blocks = SEQUENCE_TOKENS // block_tokens
    key_f32 = key_rot.astype(jnp.float32)
    value_f32 = value_b.astype(jnp.float32)
    query_tiles_list = query_rotated.reshape(number_of_blocks, block_tokens, KEY_VALUE_HEADS, heads_per_group, HEAD_DIM)
    pos_blocks = positions.reshape(number_of_blocks, block_tokens)

    def attend_block(scan_item):
        query_blk, query_pos = scan_item
        allowed = positions[None, None, None, :] <= query_pos[None, None, :, None]
        scores = jnp.einsum('qhgd,khd->hgqk', query_blk.astype(jnp.float32), key_f32) * SCORE_SCALE
        scores = jnp.where(allowed, scores, NEG_FILL)
        row_max = lax.optimization_barrier(jnp.max(scores, axis=-1, keepdims=True))
        row_sum = lax.optimization_barrier(jnp.sum(jnp.where(allowed, jnp.exp(scores - row_max), 0.0), axis=-1, keepdims=True))
        log_norm = row_max + jnp.log(row_sum)
        prob_vals = round_trip(jnp.where(allowed, jnp.exp(scores - log_norm), 0.0))
        attention_output = jnp.einsum('hgqk,khd->qhgd', prob_vals, value_f32)
        return (attention_output.astype(jnp.bfloat16), log_norm[..., 0])
    out_blocks, norm_blocks = lax.map(attend_block, (query_tiles_list, pos_blocks))
    return (out_blocks.reshape(SEQUENCE_TOKENS, QUERY_HEADS * HEAD_DIM), norm_blocks)

def attend_backward(query_rotated, key_rot, value_b, positions, norm_blocks, attention_output_grad, delta_rows):
    heads_per_group = QUERY_HEADS // KEY_VALUE_HEADS
    block_tokens = min(SEQUENCE_TOKENS, 512)
    number_of_blocks = SEQUENCE_TOKENS // block_tokens
    key_f32 = key_rot.astype(jnp.float32)
    value_f32 = value_b.astype(jnp.float32)
    query_tiles_list = query_rotated.reshape(number_of_blocks, block_tokens, KEY_VALUE_HEADS, heads_per_group, HEAD_DIM)
    pos_blocks = positions.reshape(number_of_blocks, block_tokens)
    gradient_blocks = attention_output_grad.reshape(number_of_blocks, block_tokens, KEY_VALUE_HEADS, heads_per_group, HEAD_DIM)

    def attend_block(state_in, scan_item):
        key_gradient, value_gradient = state_in
        query_blk, query_pos, log_norm, grad_blk, delta_blk = scan_item
        query_f32 = query_blk.astype(jnp.float32)
        grad_f32 = grad_blk.astype(jnp.float32)
        allowed = positions[None, None, None, :] <= query_pos[None, None, :, None]
        scores = jnp.einsum('qhgd,khd->hgqk', query_f32, key_f32) * SCORE_SCALE
        scores = jnp.where(allowed, scores, NEG_FILL)
        prob_vals = jnp.where(allowed, jnp.exp(scores - log_norm[..., None]), 0.0)
        prob_grad = jnp.einsum('qhgd,khd->hgqk', grad_f32, value_f32)
        score_grad = round_trip(prob_vals * (prob_grad - delta_blk[..., None]))
        query_grad = jnp.einsum('hgqk,khd->qhgd', score_grad, key_f32) * SCORE_SCALE
        key_gradient = key_gradient + jnp.einsum('hgqk,qhgd->khd', score_grad, query_f32) * SCORE_SCALE
        value_gradient = value_gradient + jnp.einsum('hgqk,qhgd->khd', round_trip(prob_vals), grad_f32)
        return ((key_gradient, value_gradient), query_grad)
    empty_key_value = jnp.zeros((SEQUENCE_TOKENS, KEY_VALUE_HEADS, HEAD_DIM), jnp.float32)
    (key_gradient, value_gradient), query_grads = lax.scan(attend_block, (empty_key_value, empty_key_value), (query_tiles_list, pos_blocks, norm_blocks, gradient_blocks, delta_rows))
    return (query_grads.reshape(SEQUENCE_TOKENS, QUERY_HEADS, HEAD_DIM), key_gradient, value_gradient)

def one_sequence(input_seq, block_perm, route_rows, route_w, cot_seq, gain_attn, w_query, key_weight, value_weight, w_out, gain_moe, w_gate, w_up, w_down):
    heads_per_group = QUERY_HEADS // KEY_VALUE_HEADS
    block_tokens = min(SEQUENCE_TOKENS, 512)
    number_of_blocks = SEQUENCE_TOKENS // block_tokens
    row_ids = jnp.arange(SEQUENCE_TOKENS, dtype=jnp.int32)
    positions = (block_perm[row_ids // CTX_TOK] * CTX_TOK + row_ids % CTX_TOK).astype(jnp.int32)
    cosine_table, sine_values = rope_tables(positions)
    cosine_table = cosine_table[:, None, :]
    sine_values = sine_values[:, None, :]
    inputs = input_seq.astype(jnp.float32)
    inv_a = lax.rsqrt(lax.optimization_barrier(jnp.mean(inputs * inputs, axis=-1, keepdims=True)) + EPS)
    attention_normed = (inputs * inv_a * gain_attn.astype(jnp.float32)).astype(jnp.bfloat16)
    query_projected = jnp.dot(attention_normed, w_query, preferred_element_type=jnp.float32).reshape(SEQUENCE_TOKENS, QUERY_HEADS, HEAD_DIM)
    key_projected = jnp.dot(attention_normed, key_weight, preferred_element_type=jnp.float32).reshape(SEQUENCE_TOKENS, KEY_VALUE_HEADS, HEAD_DIM)
    value_projected = jnp.dot(attention_normed, value_weight, preferred_element_type=jnp.float32).reshape(SEQUENCE_TOKENS, KEY_VALUE_HEADS, HEAD_DIM)
    query_rotated = apply_rotary(query_projected, cosine_table, sine_values).astype(jnp.bfloat16).reshape(SEQUENCE_TOKENS, KEY_VALUE_HEADS, heads_per_group, HEAD_DIM)
    key_rot = apply_rotary(key_projected, cosine_table, sine_values).astype(jnp.bfloat16)
    value_b = value_projected.astype(jnp.bfloat16)
    attention_output, norm_blocks = attend_forward(query_rotated, key_rot, value_b, positions)
    mid = inputs + RESIDUAL_SCALE * jnp.dot(attention_output, w_out, preferred_element_type=jnp.float32)
    inv_b = lax.rsqrt(lax.optimization_barrier(jnp.mean(mid * mid, axis=-1, keepdims=True)) + EPS)
    gain_b = gain_moe.astype(jnp.float32)
    normed_b = (mid * inv_b * gain_b).astype(jnp.bfloat16)
    capacity = N_CTX * CAP
    slot_of, slot_owner = expert_slots(route_rows, capacity)
    padded = jnp.concatenate([normed_b, jnp.zeros((1, MODEL_DIM), jnp.bfloat16)], axis=0)
    tiles = padded[slot_owner].reshape(LOCAL_EXPERTS, capacity, MODEL_DIM).astype(jnp.float32)
    gate_f32 = w_gate.astype(jnp.float32)
    up_f32 = w_up.astype(jnp.float32)
    down_f32 = w_down.astype(jnp.float32)
    gate_pre = jnp.einsum('ecd,edf->ecf', tiles, gate_f32)
    up_pre = jnp.einsum('ecd,edf->ecf', tiles, up_f32)
    hidden_act = round_trip(jax.nn.silu(gate_pre) * up_pre)
    expert_out = jnp.einsum('ecf,efd->ecd', hidden_act, down_f32).reshape(LOCAL_EXPERTS * capacity, MODEL_DIM)
    weights_f32 = route_w.astype(jnp.float32)
    moe = lax.optimization_barrier(jnp.sum(expert_out[slot_of] * weights_f32[..., None], axis=1))
    block_out = (mid + RESIDUAL_SCALE * moe).astype(jnp.bfloat16)
    cot_f32 = cot_seq.astype(jnp.float32)
    slot_weight = jnp.zeros((LOCAL_EXPERTS * capacity,), jnp.float32).at[slot_of.reshape(-1)].set(weights_f32.reshape(-1))
    cot_pad = jnp.concatenate([cot_f32, jnp.zeros((1, MODEL_DIM), jnp.float32)], axis=0)
    slot_grad = round_trip(slot_weight[:, None] * RESIDUAL_SCALE * cot_pad[slot_owner]).reshape(LOCAL_EXPERTS, capacity, MODEL_DIM)
    act_grad = jnp.einsum('ecd,efd->ecf', slot_grad, down_f32)
    sigmoid_z = jax.nn.sigmoid(gate_pre)
    gate_grad = round_trip(act_grad * up_pre * sigmoid_z * (1.0 + gate_pre * (1.0 - sigmoid_z)))
    up_grad = round_trip(act_grad * gate_pre * sigmoid_z)
    tile_grad = (jnp.einsum('ecf,edf->ecd', gate_grad, gate_f32) + jnp.einsum('ecf,edf->ecd', up_grad, up_f32)).reshape(LOCAL_EXPERTS * capacity, MODEL_DIM)
    normed_b_grad = lax.optimization_barrier(jnp.sum(tile_grad[slot_of], axis=1))
    grad_gate = jnp.einsum('ecd,ecf->edf', tiles, gate_grad)
    grad_up = jnp.einsum('ecd,ecf->edf', tiles, up_grad)
    grad_down = jnp.einsum('ecf,ecd->efd', hidden_act, slot_grad)
    scaled_b = gain_b * normed_b_grad
    grad_gain_moe = lax.optimization_barrier(jnp.sum(normed_b_grad * mid * inv_b, axis=0))
    mid_grad = cot_f32 + inv_b * scaled_b - mid * inv_b * inv_b * inv_b * lax.optimization_barrier(jnp.mean(scaled_b * mid, axis=-1, keepdims=True))
    mid_grad_b = (RESIDUAL_SCALE * mid_grad).astype(jnp.bfloat16)
    grad_out = jnp.dot(attention_output.T, mid_grad_b, preferred_element_type=jnp.float32)
    attention_output_grad = jnp.dot(mid_grad_b, w_out.T, preferred_element_type=jnp.float32).astype(jnp.bfloat16)
    delta_rows = lax.optimization_barrier(jnp.sum(attention_output_grad.astype(jnp.float32).reshape(SEQUENCE_TOKENS, KEY_VALUE_HEADS, heads_per_group, HEAD_DIM) * attention_output.astype(jnp.float32).reshape(SEQUENCE_TOKENS, KEY_VALUE_HEADS, heads_per_group, HEAD_DIM), axis=-1))
    delta_rows = delta_rows.reshape(number_of_blocks, block_tokens, KEY_VALUE_HEADS, heads_per_group).transpose(0, 2, 3, 1)
    query_grad, key_gradient, value_gradient = attend_backward(query_rotated, key_rot, value_b, positions, norm_blocks, attention_output_grad, delta_rows)
    query_pre = inverse_rotary(query_grad, cosine_table, sine_values).astype(jnp.bfloat16).reshape(SEQUENCE_TOKENS, QUERY_HEADS * HEAD_DIM)
    key_unrotated = inverse_rotary(key_gradient, cosine_table, sine_values).astype(jnp.bfloat16).reshape(SEQUENCE_TOKENS, KEY_VALUE_HEADS * HEAD_DIM)
    value_unprojected = value_gradient.astype(jnp.bfloat16).reshape(SEQUENCE_TOKENS, KEY_VALUE_HEADS * HEAD_DIM)
    normed_a_grad = jnp.dot(query_pre, w_query.T, preferred_element_type=jnp.float32) + jnp.dot(key_unrotated, key_weight.T, preferred_element_type=jnp.float32) + jnp.dot(value_unprojected, value_weight.T, preferred_element_type=jnp.float32)
    grad_query = jnp.dot(attention_normed.T, query_pre, preferred_element_type=jnp.float32)
    grad_key = jnp.dot(attention_normed.T, key_unrotated, preferred_element_type=jnp.float32)
    grad_value = jnp.dot(attention_normed.T, value_unprojected, preferred_element_type=jnp.float32)
    gain_a = gain_attn.astype(jnp.float32)
    scaled_a = gain_a * normed_a_grad
    grad_gain_attn = lax.optimization_barrier(jnp.sum(normed_a_grad * inputs * inv_a, axis=0))
    input_grad = mid_grad + inv_a * scaled_a - inputs * inv_a * inv_a * inv_a * lax.optimization_barrier(jnp.mean(scaled_a * inputs, axis=-1, keepdims=True))
    grad_set = (grad_gain_attn, grad_query, grad_key, grad_value, grad_out, grad_gain_moe, grad_gate, grad_up, grad_down)
    return (block_out, input_grad, grad_set)

def reference(block_input, cotangent, block_order, routes, route_weights, gain_attn, w_query, key_weight, value_weight, w_out, gain_moe, w_gate, w_up, w_down):
    initial_state = (jnp.zeros((MODEL_DIM,), jnp.float32), jnp.zeros((MODEL_DIM, QUERY_HEADS * HEAD_DIM), jnp.float32), jnp.zeros((MODEL_DIM, KEY_VALUE_HEADS * HEAD_DIM), jnp.float32), jnp.zeros((MODEL_DIM, KEY_VALUE_HEADS * HEAD_DIM), jnp.float32), jnp.zeros((QUERY_HEADS * HEAD_DIM, MODEL_DIM), jnp.float32), jnp.zeros((MODEL_DIM,), jnp.float32), jnp.zeros((LOCAL_EXPERTS, MODEL_DIM, EXPERT_HIDDEN), jnp.float32), jnp.zeros((LOCAL_EXPERTS, MODEL_DIM, EXPERT_HIDDEN), jnp.float32), jnp.zeros((LOCAL_EXPERTS, EXPERT_HIDDEN, MODEL_DIM), jnp.float32))

    def per_sequence(state_in, scan_item):
        input_seq, cot_seq, block_perm, route_rows, route_w = scan_item
        block_out, input_grad, grad_set = one_sequence(input_seq, block_perm, route_rows, route_w, cot_seq, gain_attn, w_query, key_weight, value_weight, w_out, gain_moe, w_gate, w_up, w_down)
        summed = tuple((running + fresh for running, fresh in zip(state_in, grad_set)))
        return (summed, (block_out, input_grad))
    totals, (outputs, input_grads) = lax.scan(per_sequence, initial_state, (block_input, cotangent, block_order, routes, route_weights))
    return (outputs, input_grads, totals[0], totals[1], totals[2], totals[3], totals[4], totals[5], totals[6], totals[7], totals[8])
```

```python
import jax
import jax.numpy as jnp
from jax import lax
from jax.sharding import PartitionSpec as P

HEAD_DIM = 64
TOPK = 8
EPS = 1e-06
SCORE_SCALE = 1.0 / 64.0
RESIDUAL_SCALE = 0.22
THETA = 10000.0
NEG_FILL = -1e30
BF = jnp.bfloat16
F32 = jnp.float32


def swap(value, axis, bit):
    size = lax.axis_size(axis)
    return lax.ppermute(value, axis, [(i, i ^ bit) for i in range(size)])


def after(value, token):
    return lax.optimization_barrier((value, token))[0]


def dot(a, b, dims):
    return lax.dot_general(a, b, (dims, ((), ())), preferred_element_type=F32)


def take(value, index, size, dim=0):
    return lax.dynamic_slice_in_dim(value, index * size, size, dim)


def join(own, other, bit, dim=0):
    size = own.shape[dim]
    shape = own.shape[:dim] + (2 * size,) + own.shape[dim + 1 :]
    out = lax.dynamic_update_slice_in_dim(jnp.zeros(shape, own.dtype), own, bit * size, dim)
    return lax.dynamic_update_slice_in_dim(out, other, (1 - bit) * size, dim)


def rope_tables(positions):
    half_dim = HEAD_DIM // 2
    exponent = jnp.arange(half_dim, dtype=F32) * (2.0 / HEAD_DIM)
    frequency = THETA ** (-exponent)
    angles = positions.astype(F32)[..., None] * frequency
    return (jnp.cos(angles)[:, :, None, :], jnp.sin(angles)[:, :, None, :])


def rotate(values, cos, sin):
    half = HEAD_DIM // 2
    a, b = values[..., :half], values[..., half:]
    return jnp.concatenate([a * cos - b * sin, b * cos + a * sin], axis=-1)


def group_gather(block):
    rows = block.shape[0] // 2
    a, b = block[:rows], block[rows:]
    a_x = swap(a, "seq", 1)
    b_z = swap(b, "ctx", 2)
    a = jnp.concatenate([a, a_x], 0)
    b = jnp.concatenate([b, b_z], 0)
    a_z = swap(a, "ctx", 2)
    b_x = swap(b, "seq", 1)
    both = jnp.concatenate([a, a_z, b, b_x], 0)
    return jnp.concatenate([both, swap(both, "ctx", 1)], 0)


def group_scatter(partial):
    half = partial.shape[0] // 2
    both = partial[:half] + swap(partial[half:].astype(BF), "ctx", 1).astype(F32)
    q = both.shape[0] // 4
    a_keep, a_send, b_keep, b_send = (both[i * q : (i + 1) * q] for i in range(4))
    a = a_keep + swap(a_send.astype(BF), "ctx", 2).astype(F32)
    b = b_keep + swap(b_send.astype(BF), "seq", 1).astype(F32)
    q = q // 2
    a = a[:q] + swap(a[q:].astype(BF), "seq", 1).astype(F32)
    b = b[:q] + swap(b[q:].astype(BF), "ctx", 2).astype(F32)
    return jnp.concatenate([a, b], 0)


def ctx_bits():
    size = lax.axis_size("ctx")
    bits = []
    while size > 1:
        size //= 2
        bits.append(size)
    return bits


def halve(value, axis, bit, dim=0):
    mine = (lax.axis_index(axis) // bit) % 2
    size = value.shape[dim] // 2
    sent = swap(take(value, 1 - mine, size, dim).astype(BF), axis, bit)
    return take(value, mine, size, dim).astype(F32) + sent.astype(F32)


def double(value, axis, bit, dim=0):
    mine = (lax.axis_index(axis) // bit) % 2
    return join(value, swap(value, axis, bit), mine, dim)


def reduce_grad(value, seq_dim):
    value = halve(value, "ctx", 1, 1 - seq_dim)
    value = halve(value, "seq", 1, seq_dim)
    high = ctx_bits()[:-1]
    for bit in reversed(high):
        value = halve(value, "ctx", bit, 0)
    value = value.astype(BF)
    for bit in high:
        value = double(value, "ctx", bit, 0)
    return double(value, "ctx", 1, 1 - seq_dim).astype(F32)


def per_device(
    block_input,
    cotangent,
    block_order,
    routes,
    route_weights,
    gain_attn,
    w_query,
    key_weight,
    value_weight,
    w_out,
    gain_moe,
    w_gate,
    w_up,
    w_down,
):
    seqs, rows, width = block_input.shape
    tokens = seqs * rows
    n_ctx = lax.axis_size("ctx")
    ctx = lax.axis_index("ctx")
    s_idx = lax.axis_index("seq")
    core = ctx % 2
    bits = ctx_bits()
    local_experts = w_gate.shape[0]
    n_experts = local_experts * lax.axis_size("seq")
    hidden = w_gate.shape[2]

    w_qkv = jnp.concatenate([w_query, key_weight, value_weight], 1)
    gains = jnp.stack([gain_attn, gain_moe])
    gains = join(gains, swap(gains, "seq", 1), s_idx, 1).astype(F32)
    gain_a, gain_b = gains[0], gains[1]

    def fetch(weight, dim):
        size = weight.shape[0] // 2
        half = swap(take(weight, core, size), "seq", 1)
        other = join(half, swap(half, "ctx", 1), core, 0)
        return join(weight, other, s_idx, dim)

    qkv_full = fetch(w_qkv, 0)

    offsets = [0]
    gathered = block_input
    for bit in bits:
        gathered = jnp.concatenate([gathered, swap(gathered, "ctx", bit)], 1)
        offsets = offsets + [o ^ bit for o in offsets]
    out_full = fetch(after(w_out, qkv_full), 1)

    order = jnp.stack([jnp.take(block_order, ctx ^ o, axis=1) for o in offsets], 1)
    key_pos = (
        order[:, :, None] * rows + jnp.arange(rows, dtype=jnp.int32)[None, None, :]
    ).reshape(seqs, n_ctx * rows)
    query_pos = key_pos[:, :rows]
    cos_all, sin_all = rope_tables(key_pos)
    cos_own, sin_own = cos_all[:, :rows], sin_all[:, :rows]

    q_cols = w_query.shape[1]
    kv_cols = key_weight.shape[1]
    kv_heads = kv_cols // HEAD_DIM
    group = q_cols // kv_cols

    x_all = gathered.astype(F32)
    inv_all = lax.rsqrt(jnp.mean(x_all * x_all, axis=-1, keepdims=True) + EPS)
    normed_all = (x_all * inv_all * gain_a).astype(BF)
    normed_own = normed_all[:, :rows].reshape(tokens, width)
    inputs = block_input.astype(F32).reshape(tokens, width)
    inv_a = inv_all[:, :rows].reshape(tokens, 1)

    q_proj = dot(normed_own, qkv_full[:, :q_cols], ((1,), (0,)))
    kv_proj = dot(
        normed_all.reshape(seqs * n_ctx * rows, width), qkv_full[:, q_cols:], ((1,), (0,))
    )
    query_rot = (
        rotate(q_proj.reshape(seqs, rows, kv_heads * group, HEAD_DIM), cos_own, sin_own)
        .astype(BF)
        .reshape(seqs, rows, kv_heads, group, HEAD_DIM)
    )
    keys = rotate(
        kv_proj[:, :kv_cols].reshape(seqs, n_ctx * rows, kv_heads, HEAD_DIM), cos_all, sin_all
    ).astype(BF)
    values = kv_proj[:, kv_cols:].astype(BF).reshape(seqs, n_ctx * rows, kv_heads, HEAD_DIM)

    allowed = key_pos[:, None, None, None, :] <= query_pos[:, None, None, :, None]
    scores = (
        jnp.einsum("sqhgd,skhd->shgqk", query_rot, keys, preferred_element_type=F32) * SCORE_SCALE
    )
    scores = jnp.where(allowed, scores, NEG_FILL)
    top = jnp.max(scores, axis=-1, keepdims=True)
    weights = jnp.exp(scores - top)
    total = jnp.sum(weights, axis=-1, keepdims=True)
    probs = weights / total
    probs_b = probs.astype(BF)
    attended = (
        jnp.einsum("shgqk,skhd->sqhgd", probs_b, values, preferred_element_type=F32)
        .astype(BF)
        .reshape(tokens, q_cols)
    )
    part = dot(attended, out_full, ((1,), (0,))).astype(BF)
    mid = inputs + RESIDUAL_SCALE * (part.astype(F32) + swap(part, "tensor", 1).astype(F32))
    inv_b = lax.rsqrt(jnp.mean(mid * mid, axis=-1, keepdims=True) + EPS)
    normed_b = (mid * inv_b * gain_b).astype(BF)

    sub = min(4, n_ctx)
    mine_experts = local_experts // sub
    first = (ctx % sub) * mine_experts
    gate_w, up_w, down_w = (
        lax.dynamic_slice_in_dim(w, first, mine_experts, 0) for w in (w_gate, w_up, w_down)
    )
    route_flat = routes.reshape(tokens, TOPK)
    rw = route_weights.astype(F32).reshape(tokens, TOPK)
    dense = jnp.sum(
        jnp.where(
            route_flat[:, :, None] == jnp.arange(n_experts, dtype=jnp.int32)[None, None, :],
            rw[:, :, None],
            0.0,
        ),
        axis=1,
    ).astype(BF)
    cot_in, dense_in = lax.optimization_barrier(
        (cotangent.reshape(tokens, width), dense, gathered)
    )[:2]
    cot_group = group_gather(cot_in)
    dense_group = group_gather(dense_in)
    picked = lax.dynamic_slice_in_dim(
        dense_group, s_idx * local_experts + first, mine_experts, 1
    ).astype(F32)
    norm_group = group_gather(normed_b)

    def spread(column):
        return jnp.concatenate(
            [jnp.broadcast_to(column[:, e : e + 1], (column.shape[0], hidden)) for e in range(mine_experts)],
            1,
        )

    def cols(weight):
        return jnp.concatenate([weight[e] for e in range(mine_experts)], 1)

    w_slot = spread(picked)
    gate_c, up_c = cols(gate_w), cols(up_w)
    down_r = down_w.reshape(mine_experts * hidden, width)
    act_grad = RESIDUAL_SCALE * w_slot * dot(cot_group, down_r, ((1,), (1,)))
    gate_pre = dot(norm_group, gate_c, ((1,), (0,)))
    up_pre = dot(norm_group, up_c, ((1,), (0,)))
    sig = jax.nn.sigmoid(gate_pre)
    silu = gate_pre * sig
    hidden_w = (w_slot * silu * up_pre).astype(BF)
    gate_grad = (act_grad * up_pre * sig * (1.0 + gate_pre * (1.0 - sig))).astype(BF)
    up_grad = (act_grad * silu).astype(BF)
    nb_part = dot(gate_grad, gate_c, ((1,), (1,))) + dot(up_grad, up_c, ((1,), (1,)))
    nb_sum = group_scatter(nb_part).astype(BF)
    nb_grad = nb_sum.astype(F32) + swap(nb_sum, "tensor", 1).astype(F32)
    moe_part = dot(hidden_w, down_r, ((1,), (0,)))

    pack_a = jnp.concatenate([gate_grad, up_grad], 1)

    def grads_of(index, size):
        xs = lax.dynamic_slice_in_dim(norm_group, index * size, size, 1)
        cs = lax.dynamic_slice_in_dim(cot_group, index * size, size, 1)
        return jnp.concatenate(
            [
                dot(xs, pack_a, ((0,), (0,))),
                RESIDUAL_SCALE * dot(cs, hidden_w, ((0,), (0,))),
            ],
            1,
        )

    high = [b for b in bits if b >= 4]
    if high:
        mine = (ctx // high[0]) % 2
        sent = swap(grads_of(1 - mine, width // 2).astype(BF), "ctx", high[0])
        summed = grads_of(mine, width // 2) + sent.astype(F32)
        for bit in high[1:]:
            summed = halve(summed, "ctx", bit, 0)
    else:
        summed = grads_of(0, width)
    slab = width // n_ctx
    summed_b = summed.astype(BF)
    n_cols = summed.shape[1]
    pieces = jnp.zeros((sub, slab, n_cols), BF)
    here = ctx % sub
    for r in range(sub):
        chunk = lax.dynamic_slice_in_dim(summed_b, (here ^ r) * slab, slab, 0)
        got = chunk if r == 0 else swap(chunk, "ctx", r)
        pieces = lax.dynamic_update_slice_in_dim(pieces, got[None], here ^ r, 0)
    pieces = pieces.reshape(sub, slab, 3, mine_experts, hidden)
    grad_gate, grad_up, grad_down = (
        pieces[:, :, i].transpose(0, 2, 1, 3).reshape(local_experts, slab, hidden).astype(F32)
        for i in range(3)
    )
    grad_down = grad_down.transpose(0, 2, 1)

    cot = cotangent.reshape(tokens, width).astype(F32)
    scaled_b = gain_b * nb_grad
    gain_b_part = jnp.sum(nb_grad * mid * inv_b, axis=0)
    mid_grad = (
        cot
        + inv_b * scaled_b
        - mid * inv_b * inv_b * inv_b * jnp.mean(scaled_b * mid, axis=-1, keepdims=True)
    )
    mid_grad_b = (RESIDUAL_SCALE * mid_grad).astype(BF)
    grad_out = reduce_grad(dot(attended, mid_grad_b, ((0,), (0,))), 1)
    att_grad = dot(mid_grad_b, out_full, ((1,), (1,))).astype(BF)
    grad_heads = att_grad.reshape(seqs, rows, kv_heads, group, HEAD_DIM)
    delta = jnp.sum(
        grad_heads.astype(F32)
        * attended.reshape(seqs, rows, kv_heads, group, HEAD_DIM).astype(F32),
        axis=-1,
    ).transpose(0, 2, 3, 1)
    prob_grad = jnp.einsum("sqhgd,skhd->shgqk", grad_heads, values, preferred_element_type=F32)
    score_grad = (probs * (prob_grad - delta[..., None])).astype(BF)
    query_grad = (
        jnp.einsum("shgqk,skhd->sqhgd", score_grad, keys, preferred_element_type=F32) * SCORE_SCALE
    )
    key_grad = (
        jnp.einsum("shgqk,sqhgd->skhd", score_grad, query_rot, preferred_element_type=F32)
        * SCORE_SCALE
    )
    value_grad = jnp.einsum("shgqk,sqhgd->skhd", probs_b, grad_heads, preferred_element_type=F32)
    query_pre = (
        rotate(query_grad.reshape(seqs, rows, kv_heads * group, HEAD_DIM), cos_own, -sin_own)
        .astype(BF)
        .reshape(tokens, q_cols)
    )
    kv_pre = jnp.concatenate(
        [
            rotate(key_grad, cos_all, -sin_all).reshape(seqs, n_ctx * rows, kv_cols),
            value_grad.reshape(seqs, n_ctx * rows, kv_cols),
        ],
        -1,
    )
    grad_qkv = jnp.concatenate(
        [
            dot(normed_own, query_pre, ((0,), (0,))),
            dot(
                normed_all.reshape(seqs * n_ctx * rows, width),
                kv_pre.astype(BF).reshape(seqs * n_ctx * rows, 2 * kv_cols),
                ((0,), (0,)),
            ),
        ],
        1,
    )
    gain_a_part = jnp.sum(grad_qkv * qkv_full.astype(F32), axis=1) / gain_a
    gain_parts = jnp.stack([gain_a_part, gain_b_part])
    gain_parts = gain_parts.at[1].multiply(0.5)
    gain_parts = gain_parts + swap(gain_parts, "tensor", 1)
    for bit in reversed(bits):
        gain_parts = gain_parts + swap(gain_parts, "ctx", bit)
    half_w = width // 2
    gain_sum = take(gain_parts, s_idx, half_w, 1) + swap(
        take(gain_parts, 1 - s_idx, half_w, 1), "seq", 1
    )

    own_kv = kv_pre
    for bit in reversed(bits):
        half = own_kv.shape[1] // 2
        own_kv = own_kv[:, :half] + swap(own_kv[:, half:].astype(BF), "ctx", bit).astype(F32)
    qkv_pre = jnp.concatenate([query_pre, own_kv.astype(BF).reshape(tokens, 2 * kv_cols)], 1)
    na_part = dot(qkv_pre, qkv_full, ((1,), (1,))).astype(BF)
    na_grad = na_part.astype(F32) + swap(na_part, "tensor", 1).astype(F32)
    scaled_a = gain_a * na_grad
    input_grad = (
        mid_grad
        + inv_a * scaled_a
        - inputs * inv_a * inv_a * inv_a * jnp.mean(scaled_a * inputs, axis=-1, keepdims=True)
    )
    grad_qkv = reduce_grad(grad_qkv, 0)

    moe_sum = group_scatter(after(moe_part, nb_sum)).astype(BF)
    moe = moe_sum.astype(F32) + swap(moe_sum, "tensor", 1).astype(F32)
    block_output = (mid + RESIDUAL_SCALE * moe).astype(BF)
    shape = (seqs, rows, width)
    return (
        block_output.reshape(shape),
        input_grad.reshape(shape),
        gain_sum[0],
        grad_qkv[:, :q_cols],
        grad_qkv[:, q_cols : q_cols + kv_cols],
        grad_qkv[:, q_cols + kv_cols :],
        grad_out,
        gain_sum[1],
        grad_gate,
        grad_up,
        grad_down,
    )


def solution(mesh):
    in_specs = (
        P("seq", "ctx", None),
        P("seq", "ctx", None),
        P("seq", None),
        P("seq", "ctx", None),
        P("seq", "ctx", None),
        P("seq"),
        P("seq", "tensor"),
        P("seq", "tensor"),
        P("seq", "tensor"),
        P("tensor", "seq"),
        P("seq"),
        P("seq", None, "tensor"),
        P("seq", None, "tensor"),
        P("seq", "tensor", None),
    )
    out_specs = (
        P("seq", "ctx", None),
        P("seq", "ctx", None),
        P("seq"),
        P("seq", "tensor"),
        P("seq", "tensor"),
        P("seq", "tensor"),
        P("tensor", "seq"),
        P("seq"),
        P("seq", "ctx", "tensor"),
        P("seq", "ctx", "tensor"),
        P("seq", "tensor", "ctx"),
    )
    return jax.shard_map(
        per_device, mesh=mesh, in_specs=in_specs, out_specs=out_specs, check_vma=False
    )
```

```python
import functools

import jax
import jax.numpy as jnp
from jax import lax
from jax.experimental import pallas as pl
from jax.experimental.pallas import tpu as pltpu
from jax.sharding import PartitionSpec as P

HEAD_DIM = 64
TOPK = 8
EPS = 1e-06
SCORE_SCALE = 1.0 / 64.0
RESIDUAL_SCALE = 0.22
THETA = 10000.0
NEG_FILL = -1e30
BF = jnp.bfloat16
F32 = jnp.float32
LANES = 128


def swap(value, axis, bit):
    size = lax.axis_size(axis)
    with jax.named_scope(f"swap_{axis}{bit}"):
        return lax.ppermute(value, axis, [(i, i ^ bit) for i in range(size)])


def after(value, *tokens):
    return lax.optimization_barrier((value,) + tokens)[0]


def dot(a, b, dims):
    return lax.dot_general(a, b, (dims, ((), ())), preferred_element_type=F32)


def f32(value):
    return value.astype(F32)


def shape(dims, dtype):
    return jax.ShapeDtypeStruct(dims, dtype)


def kernel(name, body, outs, scalars, arrays, scratch=(), picks=()):
    whole = pl.BlockSpec(memory_space=pltpu.VMEM)
    specs = [whole] * len(arrays)
    for array, block, which in picks:
        rest = (0,) * (len(block) - 1)
        specs.append(pl.BlockSpec(block, lambda i, ids, w=which, z=rest: (ids[w],) + z))
    return pl.pallas_call(
        body,
        name=name,
        out_shape=outs,
        grid_spec=pltpu.PrefetchScalarGridSpec(
            num_scalar_prefetch=1,
            grid=(1,),
            in_specs=specs,
            out_specs=[whole] * len(outs),
            scratch_shapes=list(scratch),
        ),
        compiler_params=pltpu.CompilerParams(vmem_limit_bytes=60 * 1024 * 1024),
    )(scalars, *arrays, *[p[0] for p in picks])


def rope(values, cos, sin):
    lane = lax.broadcasted_iota(jnp.int32, cos.shape, 1)
    first = (lane % HEAD_DIM) < HEAD_DIM // 2
    out = []
    for at in range(0, values.shape[1], LANES):
        part = values[:, at : at + LANES]
        other = jnp.where(
            first,
            pltpu.roll(part, LANES - HEAD_DIM // 2, 1),
            pltpu.roll(part, HEAD_DIM // 2, 1),
        )
        out.append(part * cos + other * sin)
    return jnp.concatenate(out, 1)


def heads_of(ref, rows, group, first):
    return jnp.concatenate(
        [ref[rows, (first + g) * HEAD_DIM : (first + g + 1) * HEAD_DIM] for g in range(group)], 0
    )


def soft(query, keys, kpos, qpos, group):
    allowed = kpos <= jnp.concatenate([qpos] * group, 0)
    scores = jnp.where(allowed, dot(query, keys, ((1,), (1,))) * SCORE_SCALE, NEG_FILL)
    weights = jnp.exp(scores - jnp.max(scores, axis=1, keepdims=True))
    return weights / jnp.sum(weights, axis=1, keepdims=True)


def forward_body(nb, seqs, rows, group, ids, *refs):
    xs, refs = refs[:nb], refs[nb:]
    wq, wk, wv, wp, wr, wo, wop, wor, gain, cos, sin, kpos, qpos = refs[:13]
    normed, w_full, wo_full, q_out, k_out, v_out, att, part = refs[13:]
    s, c = ids[0], ids[1]
    tokens, keys = seqs * rows, nb * rows
    half, quarter = wq.shape[0], wp.shape[0]
    qc, kc = wq.shape[1], wk.shape[1]
    own = pl.ds(pl.multiple_of(s * half, half), half)
    w_full[own, :qc] = wq[...]
    w_full[own, qc : qc + kc] = wk[...]
    w_full[own, qc + kc :] = wv[...]
    there = (1 - s) * half
    w_full[pl.ds(pl.multiple_of(there + c * quarter, quarter), quarter), :] = wp[...]
    w_full[pl.ds(pl.multiple_of(there + (1 - c) * quarter, quarter), quarter), :] = wr[...]
    ow, oq = wo.shape[1], wop.shape[0]
    wo_full[:, pl.ds(pl.multiple_of(s * ow, ow), ow)] = wo[...]
    cols = pl.ds(pl.multiple_of((1 - s) * ow, ow), ow)
    wo_full[pl.ds(pl.multiple_of(c * oq, oq), oq), cols] = wop[...]
    wo_full[pl.ds(pl.multiple_of((1 - c) * oq, oq), oq), cols] = wor[...]
    for r in range(nb):
        x = f32(xs[r][...])
        inv = lax.rsqrt(jnp.mean(x * x, axis=1, keepdims=True) + EPS)
        n = (x * inv * gain[...]).astype(BF)
        here = slice(r * tokens, (r + 1) * tokens)
        normed[here, :] = n
        kv = dot(n, w_full[:, qc:], ((1,), (0,)))
        k = rope(kv[:, :kc], cos[here, :], sin[here, :]).astype(BF)
        v = kv[:, kc:].astype(BF)
        for q in range(seqs):
            to = slice(q * keys + r * rows, q * keys + (r + 1) * rows)
            k_out[to, :] = k[q * rows : (q + 1) * rows]
            v_out[to, :] = v[q * rows : (q + 1) * rows]
    q_all = dot(normed[:tokens, :], w_full[:, :qc], ((1,), (0,)))
    q_out[...] = rope(q_all, cos[:tokens, :], sin[:tokens, :]).astype(BF)
    for q in range(seqs):
        mine = slice(q * rows, (q + 1) * rows)
        theirs = slice(q * keys, (q + 1) * keys)
        for h in range(kc // HEAD_DIM):
            lanes = slice(h * HEAD_DIM, (h + 1) * HEAD_DIM)
            p = soft(
                heads_of(q_out, mine, group, h * group),
                k_out[theirs, lanes],
                kpos[q : q + 1, :],
                qpos[mine, :],
                group,
            )
            o = dot(p.astype(BF), v_out[theirs, lanes], ((1,), (0,))).astype(BF)
            for g in range(group):
                at = (h * group + g) * HEAD_DIM
                att[mine, at : at + HEAD_DIM] = o[g * rows : (g + 1) * rows]
    part[...] = dot(att[...], wo_full[...], ((1,), (0,))).astype(BF)


def mid_body(ids, x, part, other, gain, mid, normed):
    m = f32(x[...]) + RESIDUAL_SCALE * (f32(part[...]) + f32(other[...]))
    mid[...] = m
    inv = lax.rsqrt(jnp.mean(m * m, axis=1, keepdims=True) + EPS)
    normed[...] = (m * inv * gain[...]).astype(BF)


def act_body(nb, mine, hidden, width, ids, *refs):
    cots, refs = refs[:nb], refs[nb:]
    down, act, wsel = refs
    tokens = cots[0].shape[0]
    for r in range(nb):
        here = slice(r * tokens, (r + 1) * tokens)
        dense = f32(cots[r][:, width:])
        lane = lax.broadcasted_iota(jnp.int32, dense.shape, 1)
        for e in range(mine):
            w = jnp.sum(jnp.where(lane == ids[1] + e, dense, 0.0), axis=1, keepdims=True)
            wsel[here, e * LANES : (e + 1) * LANES] = jnp.broadcast_to(w, (tokens, LANES))
            a = dot(cots[r][:, :width], down[e], ((1,), (1,)))
            act[here, e * hidden : (e + 1) * hidden] = (RESIDUAL_SCALE * w) * a


def expert_body(nb, mine, hidden, ids, *refs):
    norms, refs = refs[:nb], refs[nb:]
    act, wsel, gate, up, grads, hid, keep, send = refs
    tokens = norms[0].shape[0]
    for r in range(nb):
        here = slice(r * tokens, (r + 1) * tokens)
        x = norms[r][...]
        back = None
        for e in range(mine):
            g = dot(x, gate[e], ((1,), (0,)))
            u = dot(x, up[e], ((1,), (0,)))
            sig = 1.0 / (1.0 + jnp.exp(-g))
            silu = g * sig
            w = jnp.concatenate([wsel[here, e * LANES : (e + 1) * LANES]] * (hidden // LANES), 1)
            a = act[here, e * hidden : (e + 1) * hidden]
            hid[here, e * hidden : (e + 1) * hidden] = (w * silu * u).astype(BF)
            dg = (a * u * sig * (1.0 + g * (1.0 - sig))).astype(BF)
            du = (a * silu).astype(BF)
            at = e * hidden
            grads[here, at : at + hidden] = dg
            grads[here, (mine + e) * hidden : (mine + e + 1) * hidden] = du
            term = dot(dg, gate[e], ((1,), (1,))) + dot(du, up[e], ((1,), (1,)))
            back = term if back is None else back + term
        half = nb // 2
        if r < half:
            keep[here, :] = back
        else:
            send[(r - half) * tokens : (r - half + 1) * tokens, :] = back.astype(BF)


def expert_grads_body(nb, mine, hidden, width, order, slab, ids, *refs):
    norms, cots, refs = refs[:nb], refs[nb : 2 * nb], refs[2 * nb :]
    grads, hid, down, keep, send, mkeep, msend, xs, cs, full = refs
    tokens = norms[0].shape[0]
    for r in range(nb):
        here = slice(r * tokens, (r + 1) * tokens)
        xs[here, :] = norms[r][...]
        cs[here, :] = cots[r][:, :width]
    n = 2 * mine * hidden
    step = 2 * LANES
    for at in range(0, width, step):
        full[at : at + step, :n] = dot(xs[:, at : at + step], grads[...], ((0,), (0,))).astype(BF)
        full[at : at + step, n:] = (
            RESIDUAL_SCALE * dot(cs[:, at : at + step], hid[...], ((0,), (0,)))
        ).astype(BF)
    half = len(order) // 2
    for i, o in enumerate(order):
        at = pl.multiple_of((ids[2] ^ o) * slab, slab)
        if i < half or half == 0:
            keep[i * slab : (i + 1) * slab, :] = full[pl.ds(at, slab), :]
        else:
            send[(i - half) * slab : (i - half + 1) * slab, :] = full[pl.ds(at, slab), :]
    half = nb // 2
    for r in range(nb):
        here = slice(r * tokens, (r + 1) * tokens)
        out = None
        for e in range(mine):
            term = dot(hid[here, e * hidden : (e + 1) * hidden], down[e], ((1,), (0,)))
            out = term if out is None else out + term
        if r < half:
            mkeep[here, :] = out.astype(BF)
        else:
            msend[(r - half) * tokens : (r - half + 1) * tokens, :] = out.astype(BF)


def backward_body(nb, seqs, rows, group, ids, *refs):
    ins, outs = refs[:14], refs[14:]
    nb_own, nb_other, cot, mid, gain, att, q_in, k_in, v_in, kpos, qpos, cos, sin, wo = ins
    mid_grad, mgb, q_pre, keep, send, gain_part, agrad, kv, qg = outs
    tokens, keys = seqs * rows, nb * rows
    kc = k_in.shape[1]
    m = mid[...]
    inv = lax.rsqrt(jnp.mean(m * m, axis=1, keepdims=True) + EPS)
    grad = f32(nb_own[...]) + f32(nb_other[...])
    gain_part[...] = jnp.sum(grad * m * inv, axis=0, keepdims=True)
    scaled = gain[...] * grad
    mg = (
        f32(cot[...])
        + inv * scaled
        - m * inv * inv * inv * jnp.mean(scaled * m, axis=1, keepdims=True)
    )
    mid_grad[...] = mg
    mgb[...] = (RESIDUAL_SCALE * mg).astype(BF)
    agrad[...] = dot(mgb[...], wo[...], ((1,), (1,))).astype(BF)
    for q in range(seqs):
        mine = slice(q * rows, (q + 1) * rows)
        theirs = slice(q * keys, (q + 1) * keys)
        for h in range(kc // HEAD_DIM):
            lanes = slice(h * HEAD_DIM, (h + 1) * HEAD_DIM)
            query = heads_of(q_in, mine, group, h * group)
            k, v = k_in[theirs, lanes], v_in[theirs, lanes]
            p = soft(query, k, kpos[q : q + 1, :], qpos[mine, :], group)
            da = heads_of(agrad, mine, group, h * group)
            out = heads_of(att, mine, group, h * group)
            delta = jnp.sum(f32(da) * f32(out), axis=1, keepdims=True)
            ds = (p * (dot(da, v, ((1,), (1,))) - delta)).astype(BF)
            dq = dot(ds, k, ((1,), (0,))) * SCORE_SCALE
            for g in range(group):
                at = (h * group + g) * HEAD_DIM
                qg[mine, at : at + HEAD_DIM] = dq[g * rows : (g + 1) * rows]
            dk = dot(ds, query, ((0,), (0,))) * SCORE_SCALE
            dv = dot(p.astype(BF), da, ((0,), (0,)))
            for r in range(nb):
                to = slice(r * tokens + q * rows, r * tokens + (q + 1) * rows)
                kv[to, lanes] = dk[r * rows : (r + 1) * rows]
                kv[to, kc + h * HEAD_DIM : kc + (h + 1) * HEAD_DIM] = dv[
                    r * rows : (r + 1) * rows
                ]
    q_pre[...] = rope(qg[...], cos[:tokens, :], -sin[:tokens, :]).astype(BF)
    half = nb // 2
    for r in range(nb):
        here = slice(r * tokens, (r + 1) * tokens)
        out, to = (keep, here) if r < half else (
            send,
            slice((r - half) * tokens, (r - half + 1) * tokens),
        )
        out[to, :kc] = rope(kv[here, :kc], cos[here, :], -sin[here, :]).astype(BF)
        out[to, kc:] = kv[here, kc:].astype(BF)


def weight_grads_body(tokens, order, chunk, ids, *refs):
    normed, q_pre, kv_keep, kv_send, mgb, att, w_full, keep, send, gain_part, full = refs
    width = normed.shape[1]
    qc, kc2 = q_pre.shape[1], kv_keep.shape[1]
    half = kv_keep.shape[0]
    step = 2 * LANES
    for at in range(0, width, step):
        cols = slice(at, at + step)
        gq = dot(normed[:tokens, cols], q_pre[...], ((0,), (0,)))
        gkv = dot(normed[:half, cols], kv_keep[...], ((0,), (0,))) + dot(
            normed[half:, cols], kv_send[...], ((0,), (0,))
        )
        gain_part[cols, :] = jnp.sum(gq * f32(w_full[cols, :qc]), axis=1, keepdims=True) + jnp.sum(
            gkv * f32(w_full[cols, qc:]), axis=1, keepdims=True
        )
        full[cols, :qc] = gq.astype(BF)
        full[cols, qc : qc + kc2] = gkv.astype(BF)
        full[cols, qc + kc2 :] = dot(mgb[:, cols], att[...], ((0,), (0,))).astype(BF)
    s, c, z = ids[0], ids[1], ids[2] // 2
    quarter = chunk * len(order)
    for i, sx in enumerate((s, 1 - s)):
        for out, cx in ((keep, c), (send, 1 - c)):
            for j, o in enumerate(order):
                at = pl.multiple_of((sx * 2 + cx) * quarter + (z ^ (o // 2)) * chunk, chunk)
                out[i, j * chunk : (j + 1) * chunk, :] = full[pl.ds(at, chunk), :]


def back_body(ids, q_pre, kv_own, kv_other, w_full, part):
    qc = q_pre.shape[1]
    kv = (f32(kv_own[...]) + f32(kv_other[...])).astype(BF)
    part[...] = (
        dot(q_pre[...], w_full[:, :qc], ((1,), (1,))) + dot(kv, w_full[:, qc:], ((1,), (1,)))
    ).astype(BF)


def last_body(ids, x_in, mid_grad, part, other, gain, out):
    x = f32(x_in[...])
    inv = lax.rsqrt(jnp.mean(x * x, axis=1, keepdims=True) + EPS)
    scaled = gain[...] * (f32(part[...]) + f32(other[...]))
    out[...] = (
        mid_grad[...]
        + inv * scaled
        - x * inv * inv * inv * jnp.mean(scaled * x, axis=1, keepdims=True)
    )


def place_experts_body(sub, mine, hidden, ids, *refs):
    pieces, (gate, up, down) = refs[:sub], refs[sub:]
    j = ids[2] % sub
    for r in range(sub):
        for e in range(mine):
            to = (j ^ r) * mine + e
            gate[to] = f32(pieces[r][:, e * hidden : (e + 1) * hidden])
            up[to] = f32(pieces[r][:, (mine + e) * hidden : (mine + e + 1) * hidden])
            down[to] = f32(pieces[r][:, (2 * mine + e) * hidden : (2 * mine + e + 1) * hidden]).T


def place_weights_body(order, chunk, ids, own, other, gq, gk, gv, go, full):
    c, z = ids[1], ids[2] // 2
    quarter = chunk * len(order)
    for ref, cx in ((own, c), (other, 1 - c)):
        for j, o in enumerate(order):
            at = pl.multiple_of(cx * quarter + (z ^ (o // 2)) * chunk, chunk)
            full[pl.ds(at, chunk), :] = f32(ref[j * chunk : (j + 1) * chunk, :])
    qc, kc = gq.shape[1], gk.shape[1]
    gq[...] = full[:, :qc]
    gk[...] = full[:, qc : qc + kc]
    gv[...] = full[:, qc + kc : qc + 2 * kc]
    go[...] = full[:, qc + 2 * kc :].T


def group_gather(block):
    x = swap(block, "seq", 1)
    z = swap(block, "ctx", 2)
    xz = swap(x, "ctx", 2)
    near = [block, x, z, xz]
    return near + [swap(b, "ctx", 1) for b in near]


def group_scatter(keep, send):
    other = swap(send, "ctx", 1)
    rows = keep.shape[0] // 4
    part = [
        f32(keep[i * rows : (i + 1) * rows]) + f32(other[i * rows : (i + 1) * rows])
        for i in range(4)
    ]
    bits = [b.astype(BF) for b in part[1:]]
    z = swap(bits[1], "ctx", 2)
    x = swap(bits[0], "seq", 1)
    with jax.named_scope("swap_diag"):
        size = lax.axis_size("ctx")
        pairs = [(i, (i ^ size) ^ 2) for i in range(2 * size)]
        xz = lax.ppermute(bits[2], ("seq", "ctx"), pairs)
    return (part[0] + f32(x) + f32(z) + f32(xz)).astype(BF)


def per_device(
    block_input,
    cotangent,
    block_order,
    routes,
    route_weights,
    gain_attn,
    w_query,
    key_weight,
    value_weight,
    w_out,
    gain_moe,
    w_gate,
    w_up,
    w_down,
):
    seqs, rows, width = block_input.shape
    tokens = seqs * rows
    n_ctx = lax.axis_size("ctx")
    ctx = lax.axis_index("ctx")
    s_idx = lax.axis_index("seq")
    core = ctx % 2
    local_experts = w_gate.shape[0]
    n_experts = local_experts * lax.axis_size("seq")
    hidden = w_gate.shape[2]
    sub = min(4, n_ctx)
    mine = local_experts // sub
    high = []
    bit = n_ctx // 2
    while bit > 1:
        high.append(bit)
        bit //= 2
    ids = jnp.stack(
        [s_idx, core, ctx, s_idx * local_experts + (ctx % sub) * mine]
    ).astype(jnp.int32)
    pick_ids = jnp.stack([ctx % sub, ids[3], ctx]).astype(jnp.int32)

    gains = jnp.stack([gain_attn, gain_moe])
    gains_other = swap(gains, "seq", 1)
    gains = jnp.where(
        s_idx == 0,
        jnp.concatenate([gains, gains_other], 1),
        jnp.concatenate([gains_other, gains], 1),
    ).astype(F32)
    gain_a, gain_b = gains[0:1], gains[1:2]

    def half_of(weight):
        size = weight.shape[0] // 2
        return lax.dynamic_slice_in_dim(weight, core * size, size, 0)

    qkv_half = jnp.concatenate([half_of(w_query), half_of(key_weight), half_of(value_weight)], 1)
    qkv_near = swap(qkv_half, "seq", 1)
    x_own = block_input.reshape(tokens, width)
    blocks, offsets = [x_own], [0]
    for bit in high:
        blocks = blocks + [swap(b, "ctx", bit) for b in blocks]
        offsets = offsets + [o ^ bit for o in offsets]
    chunk_order = list(offsets)
    out_near = swap(after(half_of(w_out), qkv_half), "seq", 1)
    qkv_far = swap(qkv_near, "ctx", 1)
    out_far = swap(out_near, "ctx", 1)
    blocks = blocks + [swap(b, "ctx", 1) for b in blocks]
    offsets = offsets + [o ^ 1 for o in offsets]

    order = jnp.stack([jnp.take(block_order, ctx ^ o, axis=1) for o in offsets], 0)
    places = (
        order[:, :, None] * rows + jnp.arange(rows, dtype=jnp.int32)[None, None, :]
    )
    kpos = places.transpose(1, 0, 2).reshape(seqs, n_ctx * rows)
    qpos = places[0].reshape(tokens, 1)
    lane = jnp.arange(LANES, dtype=jnp.int32)
    exponent = (lane % (HEAD_DIM // 2)).astype(F32) * (2.0 / HEAD_DIM)
    angles = places.reshape(n_ctx * tokens, 1).astype(F32) * (THETA ** (-exponent))[None, :]
    cos = jnp.cos(angles)
    sin = jnp.sin(angles) * jnp.where((lane % HEAD_DIM) < HEAD_DIM // 2, -1.0, 1.0)[None, :]

    q_cols, kv_cols = w_query.shape[1], key_weight.shape[1]
    group = q_cols // kv_cols
    all_tokens = n_ctx * tokens
    normed, w_full, wo_full, q, k, v, attended, part = kernel(
        "attention_forward",
        functools.partial(forward_body, n_ctx, seqs, rows, group),
        [
            shape((all_tokens, width), BF),
            shape((width, q_cols + 2 * kv_cols), BF),
            shape((q_cols, width), BF),
            shape((tokens, q_cols), BF),
            shape((all_tokens, kv_cols), BF),
            shape((all_tokens, kv_cols), BF),
            shape((tokens, q_cols), BF),
            shape((tokens, width), BF),
        ],
        ids,
        [*blocks, w_query, key_weight, value_weight, qkv_near, qkv_far]
        + [w_out, out_near, out_far, gain_a, cos, sin, kpos, qpos],
    )

    route_flat = routes.reshape(tokens, TOPK)
    weights = f32(route_weights).reshape(tokens, TOPK)
    dense = jnp.sum(
        jnp.where(
            route_flat[:, :, None] == jnp.arange(LANES, dtype=jnp.int32)[None, None, :],
            weights[:, :, None],
            0.0,
        ),
        axis=1,
    ).astype(BF)
    cot = cotangent.reshape(tokens, width)
    cot_ext = after(jnp.concatenate([cot, dense], 1), blocks[len(high)], out_near)
    cots = group_gather(cot_ext)
    n_group = len(cots)
    group_tokens = n_group * tokens
    packed = mine * hidden
    act, wsel = kernel(
        "expert_act",
        functools.partial(act_body, n_group, mine, hidden, width),
        [shape((group_tokens, packed), F32), shape((group_tokens, mine * LANES), F32)],
        pick_ids,
        cots,
        picks=[(w_down, (mine, hidden, width), 0)],
    )

    mid, normed_b = kernel(
        "mid",
        mid_body,
        [shape((tokens, width), F32), shape((tokens, width), BF)],
        ids,
        [x_own, part, swap(part, "tensor", 1), gain_b],
    )
    norms = group_gather(normed_b)
    half_group = group_tokens // 2
    grads, hid, nb_keep, nb_send = kernel(
        "experts",
        functools.partial(expert_body, n_group, mine, hidden),
        [
            shape((group_tokens, 2 * packed), BF),
            shape((group_tokens, packed), BF),
            shape((half_group, width), F32),
            shape((half_group, width), BF),
        ],
        pick_ids,
        [*norms, act, wsel],
        picks=[(w_gate, (mine, width, hidden), 0), (w_up, (mine, width, hidden), 0)],
    )
    nb_sum = group_scatter(nb_keep, nb_send)
    nb_other = swap(nb_sum, "tensor", 1)

    slab = width // n_ctx
    far = [b for b in high if b >= 4]
    slab_order = [0]
    for bit in far:
        slab_order = slab_order + [o ^ bit for o in slab_order]
    slab_order = [o ^ r for o in slab_order for r in range(sub)]
    n_send = len(slab_order) // 2 if far else 0
    n_keep = len(slab_order) - n_send
    e_keep, e_send, m_keep, m_send = kernel(
        "expert_grads",
        functools.partial(expert_grads_body, n_group, mine, hidden, width, slab_order, slab),
        [
            shape((n_keep * slab, 3 * packed), BF),
            shape((max(n_send, 1) * slab, 3 * packed), BF),
            shape((half_group, width), BF),
            shape((half_group, width), BF),
        ],
        pick_ids,
        [*norms, *cots, grads, hid],
        scratch=[
            pltpu.VMEM((group_tokens, width), BF),
            pltpu.VMEM((group_tokens, width), BF),
            pltpu.VMEM((width, 3 * packed), BF),
        ],
        picks=[(w_down, (mine, hidden, width), 0)],
    )

    mid_grad, mgb, q_pre, kv_keep, kv_send, gain_b_part = kernel(
        "attention_backward",
        functools.partial(backward_body, n_ctx, seqs, rows, group),
        [
            shape((tokens, width), F32),
            shape((tokens, width), BF),
            shape((tokens, q_cols), BF),
            shape((all_tokens // 2, 2 * kv_cols), BF),
            shape((all_tokens // 2, 2 * kv_cols), BF),
            shape((1, width), F32),
        ],
        ids,
        [nb_sum, nb_other, cot, mid, gain_b, attended, q, k, v, kpos, qpos, cos, sin, wo_full],
        scratch=[
            pltpu.VMEM((tokens, q_cols), BF),
            pltpu.VMEM((all_tokens, 2 * kv_cols), F32),
            pltpu.VMEM((tokens, q_cols), F32),
        ],
    )

    kv = (f32(kv_keep) + f32(swap(kv_send, "ctx", 1))).astype(BF)
    low_first = list(reversed(high))
    for bit in low_first[:-1]:
        size = kv.shape[0] // 2
        kv = (f32(kv[:size]) + f32(swap(kv[size:], "ctx", bit))).astype(BF)
    size = kv.shape[0] // 2
    kv_own, kv_other = kv[:size], swap(kv[size:], "ctx", low_first[-1])

    chunk = width // (2 * n_ctx)
    quarter = width // 4
    n_cols = 2 * q_cols + 2 * kv_cols
    w_keep, w_send, gain_a_part = kernel(
        "weight_grads",
        functools.partial(weight_grads_body, tokens, chunk_order, chunk),
        [
            shape((2, quarter, n_cols), BF),
            shape((2, quarter, n_cols), BF),
            shape((width, 1), F32),
        ],
        ids,
        [normed, q_pre, kv_keep, kv_send, mgb, attended, w_full],
        scratch=[pltpu.VMEM((width, n_cols), BF)],
    )
    (na_part,) = kernel(
        "attention_input_grad",
        back_body,
        [shape((tokens, width), BF)],
        ids,
        [q_pre, kv_own, kv_other, w_full],
    )
    (input_grad,) = kernel(
        "input_grad",
        last_body,
        [shape((tokens, width), F32)],
        ids,
        [x_own, mid_grad, na_part, swap(na_part, "tensor", 1), gain_a],
    )

    w_other = swap(w_send, "ctx", 1)
    x_other = swap((f32(w_keep[1]) + f32(w_other[1])).astype(BF), "seq", 1)
    total = (f32(w_keep[0]) + f32(w_other[0]) + f32(x_other)).astype(BF)
    for bit in low_first:
        size = total.shape[0] // 2
        total = (f32(total[:size]) + f32(swap(total[size:], "ctx", bit))).astype(BF)
    for bit in high:
        total = jnp.concatenate([total, swap(total, "ctx", bit)], 0)
    half_w = width // 2
    grad_query, grad_key, grad_value, grad_out = kernel(
        "place_weights",
        functools.partial(place_weights_body, chunk_order, chunk),
        [
            shape((half_w, q_cols), F32),
            shape((half_w, kv_cols), F32),
            shape((half_w, kv_cols), F32),
            shape((q_cols, half_w), F32),
        ],
        ids,
        [total, swap(total, "ctx", 1)],
        scratch=[pltpu.VMEM((half_w, n_cols), F32)],
    )

    gain_parts = jnp.concatenate(
        [
            gain_a_part.reshape(1, width) / gain_a,
            gain_b_part * (1.0 / lax.axis_size("tensor")),
        ],
        0,
    )
    gain_parts = gain_parts + swap(gain_parts, "tensor", 1)
    for bit in [1] + low_first:
        gain_parts = gain_parts + swap(gain_parts, "ctx", bit)
    gain_sum = lax.dynamic_slice_in_dim(gain_parts, s_idx * half_w, half_w, 1) + swap(
        lax.dynamic_slice_in_dim(gain_parts, (1 - s_idx) * half_w, half_w, 1), "seq", 1
    )

    e_send = after(e_send, nb_other)
    summed = e_keep
    if far:
        summed = (f32(e_keep) + f32(swap(e_send, "ctx", far[-1]))).astype(BF)
        for bit in reversed(far[:-1]):
            size = summed.shape[0] // 2
            summed = (f32(summed[:size]) + f32(swap(summed[size:], "ctx", bit))).astype(BF)
    pieces = [summed[:slab]]
    for r in range(1, sub):
        pieces.append(swap(summed[r * slab : (r + 1) * slab], "ctx", r))
    grad_gate, grad_up, grad_down = kernel(
        "place_experts",
        functools.partial(place_experts_body, sub, mine, hidden),
        [
            shape((local_experts, slab, hidden), F32),
            shape((local_experts, slab, hidden), F32),
            shape((local_experts, hidden, slab), F32),
        ],
        ids,
        pieces,
    )

    moe_sum = group_scatter(m_keep, after(m_send, nb_other))
    block_output = (
        mid + RESIDUAL_SCALE * (f32(moe_sum) + f32(swap(moe_sum, "tensor", 1)))
    ).astype(BF)
    dims = (seqs, rows, width)
    return (
        block_output.reshape(dims),
        input_grad.reshape(dims),
        gain_sum[0],
        grad_query,
        grad_key,
        grad_value,
        grad_out,
        gain_sum[1],
        grad_gate,
        grad_up,
        grad_down,
    )


def solution(mesh):
    in_specs = (
        P("seq", "ctx", None),
        P("seq", "ctx", None),
        P("seq", None),
        P("seq", "ctx", None),
        P("seq", "ctx", None),
        P("seq"),
        P("seq", "tensor"),
        P("seq", "tensor"),
        P("seq", "tensor"),
        P("tensor", "seq"),
        P("seq"),
        P("seq", None, "tensor"),
        P("seq", None, "tensor"),
        P("seq", "tensor", None),
    )
    out_specs = (
        P("seq", "ctx", None),
        P("seq", "ctx", None),
        P("seq"),
        P("seq", "tensor"),
        P("seq", "tensor"),
        P("seq", "tensor"),
        P("tensor", "seq"),
        P("seq"),
        P("seq", "ctx", "tensor"),
        P("seq", "ctx", "tensor"),
        P("seq", "tensor", "ctx"),
    )
    return jax.shard_map(
        per_device, mesh=mesh, in_specs=in_specs, out_specs=out_specs, check_vma=False
    )
```
